32 devices in a mesh: group: 4 (over z), vf: 8 (over y, x, core).
Axes of the slice: x: 2, y: 2, z: 4, core: 2. Of those that a mesh axis runs over, the one named last changes fastest.
Arguments:
- query_rows: bfloat16 [32, 512, 1536], P(('group', 'vf')), may hold values from -28 to 28
- key_value: bfloat16 [32, 2, 512, 1536], P(('group', 'vf')), may hold values from -8 to 8
- out_weight: bfloat16 [1536, 1536], replicated, may hold values from -0.15625 to 0.15625
- partners: int32 [8, 6], replicated, may hold values from -1 to 7, as said below
Outputs:
- mixed: bfloat16 [32, 512, 1536], P(('group', 'vf'))
The draws below stay inside these ranges and needn't reach their ends.
Inputs may be any that keep to these rules, and one draw needn't show every extreme that they name: Row v lists the distinct partners of view v, each of the form (v + d) mod 8 for an offset d in -3 to 3 other than 0, followed by -1 in the slots left over; the relation is symmetric; every view has 1 to 6 partners and some view has 6.
All inputs are finite; a program needn't handle non-finite values.
Results may differ from the reference program's by a relative error of at most 0.0052.
Values may be sent and summed in bfloat16 or wider, within the bound.
A program may use at most 128 MiB of HBM per device.

```python
import math
import jax
import jax.numpy as jnp
from jax import lax

HEADS = 12
HEAD_DIM = 128
D = 1536
FRAMES = 4
TOK = 512
VIEWS = 8
VF_ALL = 32


def draw_query_rows(key, part):
    drawn_base = jnp.clip(jax.random.normal(jax.random.fold_in(key, 1), (VF_ALL, TOK, D), jnp.float32) * 1.4, -8.0, 8.0)
    return drawn_base.astype(jnp.bfloat16)


def draw_key_value(key, part):
    key_part = jnp.clip(jax.random.normal(jax.random.fold_in(key, 2), (VF_ALL, TOK, D), jnp.float32) * 1.4, -8.0, 8.0)
    value_part = jnp.clip(jax.random.normal(jax.random.fold_in(key, 3), (VF_ALL, TOK, D), jnp.float32), -6.0, 6.0)
    return jnp.stack([key_part, value_part], axis=1).astype(jnp.bfloat16)


def draw_partners(key, part):
    all_views = jnp.arange(VIEWS, dtype=jnp.int32)
    distances = jnp.arange(1, 4, dtype=jnp.int32)
    coin_flip = jax.random.randint(jax.random.fold_in(key, 11), (VIEWS, 3), 0, 8)
    centre = jax.random.randint(jax.random.fold_in(key, 12), (), 0, VIEWS)
    upper = (all_views[:, None] + distances[None, :]) % VIEWS
    forced = (distances[None, :] == 1) & (all_views[:, None] % 2 == 0) | (all_views[:, None] == centre) | (upper == centre)
    edge_on = (coin_flip > 0) | forced
    down_cols = [jnp.roll(edge_on[:, distance - 1], distance) for distance in (3, 2, 1)]
    up_cols = [edge_on[:, distance - 1] for distance in (1, 2, 3)]
    present = jnp.stack(down_cols + up_cols, axis=1)
    offsets = jnp.array([-3, -2, -1, 1, 2, 3], jnp.int32)
    ids_all = jnp.where(present, (all_views[:, None] + offsets[None, :]) % VIEWS, -1).astype(jnp.int32)
    rotate = jax.random.randint(jax.random.fold_in(key, 13), (VIEWS, 1), 0, 6)
    slot_rank = (jnp.arange(6, dtype=jnp.int32)[None, :] + rotate) % 6
    sort_keys = (1 - present.astype(jnp.int32)) * 8 + slot_rank
    order_idx = jnp.argsort(sort_keys, axis=1, stable=True)
    return jnp.take_along_axis(ids_all, order_idx, axis=1).astype(jnp.int32)


def gaussian(rng, extent, spread, reach, held_as=jnp.bfloat16):
    return jnp.clip(spread * jax.random.normal(rng, extent, jnp.float32), -reach, reach).astype(held_as)


def setup_inputs(seed: int = 0) -> dict:
    arg_keys = jax.random.split(jax.random.key(seed), 5)
    return {
        "query_rows": draw_query_rows(jax.random.fold_in(arg_keys[4], 71), 0),
        "key_value": draw_key_value(jax.random.fold_in(arg_keys[4], 71), 0),
        "out_weight": gaussian(arg_keys[2], (D, D), D ** -0.5, 0.15625),
        "partners": draw_partners(jax.random.fold_in(arg_keys[4], 71), 0),
    }


def attend(query_block, key_block, value_block):
    row_count = query_block.shape[0]
    query_heads = query_block.astype(jnp.float32).reshape(row_count, HEADS, HEAD_DIM)
    key_heads = key_block.astype(jnp.float32).reshape(key_block.shape[0], HEADS, HEAD_DIM)
    value_heads = value_block.astype(jnp.float32).reshape(value_block.shape[0], HEADS, HEAD_DIM)
    scores = jnp.einsum('qhd,khd->hqk', query_heads, key_heads) * (1.0 / math.sqrt(HEAD_DIM))
    row_max = lax.optimization_barrier(jnp.max(scores, axis=2))
    exponent = jnp.exp(scores - row_max[:, :, None])
    row_total = lax.optimization_barrier(jnp.sum(exponent, axis=2))
    rounded_probs = lax.optimization_barrier(exponent.astype(jnp.bfloat16)).astype(jnp.float32)
    weighted = jnp.einsum('hqk,khd->qhd', rounded_probs, value_heads)
    return (weighted.reshape(row_count, HEADS * HEAD_DIM), row_max, row_total)

def reference(query_rows, key_value, out_weight, partners):
    offsets = [-3, -2, -1, 1, 2, 3]

    def per_frame(frame_index):
        own_view = frame_index // FRAMES
        own_frame = frame_index % FRAMES
        query_block = query_rows[frame_index]
        listed = partners[own_view]
        blocks_list = [attend(query_block, key_value[frame_index, 0], key_value[frame_index, 1])]
        flag_list = [jnp.array(True)]
        for offset in offsets:
            partner_view = ((own_view + offset) % VIEWS).astype(jnp.int32)
            source_index = (partner_view * FRAMES + own_frame).astype(jnp.int32)
            flag_list.append(jnp.any(listed == partner_view))
            blocks_list.append(attend(query_block, key_value[source_index, 0], key_value[source_index, 1]))
        global_max = blocks_list[0][1]
        for linked_flag, block in zip(flag_list[1:], blocks_list[1:]):
            global_max = jnp.where(linked_flag, jnp.maximum(global_max, block[1]), global_max)
        summed = jnp.zeros((TOK, HEADS, HEAD_DIM), jnp.float32)
        totals = jnp.zeros((HEADS, TOK), jnp.float32)
        for linked_flag, block in zip(flag_list, blocks_list):
            weighted, row_max, row_total = block
            scale_rows = jnp.where(linked_flag, jnp.exp(row_max - global_max), 0.0).astype(jnp.float32)
            summed = summed + weighted.reshape(TOK, HEADS, HEAD_DIM) * scale_rows.T[:, :, None]
            totals = totals + row_total * scale_rows
        attended = (summed / totals.T[:, :, None]).reshape(TOK, D)
        normed = (attended * lax.rsqrt(lax.optimization_barrier(jnp.mean(attended * attended, axis=1, keepdims=True)) + 1e-06)).astype(jnp.bfloat16)
        return jnp.dot(normed, out_weight, preferred_element_type=jnp.float32).astype(jnp.bfloat16)
    return lax.map(per_frame, jnp.arange(VF_ALL, dtype=jnp.int32))
```

```python
import math

import jax
import jax.numpy as jnp
from jax import lax
from jax.experimental import pallas as pl
from jax.experimental.pallas import tpu as pltpu
from jax.sharding import PartitionSpec as P

HEADS = 12
HEAD_DIM = 128
FRAMES = 4
OFFSETS = (0, -3, -2, -1, 1, 2, 3)
SCALE = math.log2(math.e) / math.sqrt(HEAD_DIM)
FAR = 1e30
SPARE = 6 << 20
MESH = pl.DeviceIdType.MESH


def attend_rows(query, keys, values, gap, scores):
    tokens = keys(0).shape[0]
    running = None
    for b in range(len(OFFSETS)):
        block = lax.dot_general(
            query, keys(b), (((1,), (1,)), ((), ())), preferred_element_type=jnp.float32
        )
        scores[:, b * tokens : (b + 1) * tokens] = block
        lanes = block[:, :HEAD_DIM]
        for c in range(HEAD_DIM, tokens, HEAD_DIM):
            lanes = jnp.maximum(lanes, block[:, c : c + HEAD_DIM])
        running = lanes if b == 0 else jnp.maximum(running, lanes - gap(b))
    row_max = jnp.max(running, axis=1, keepdims=True) * SCALE
    total = None
    ones = jnp.ones((tokens, HEAD_DIM), jnp.bfloat16)
    for b in range(len(OFFSETS)):
        shift = row_max if b == 0 else row_max + gap(b)
        exponent = jnp.exp2(scores[:, b * tokens : (b + 1) * tokens] * SCALE - shift)
        part = jnp.dot(
            exponent.astype(jnp.bfloat16),
            jnp.concatenate([values(b), ones], axis=1),
            preferred_element_type=jnp.float32,
        )
        total = part if total is None else total + part
    return total[:, :HEAD_DIM] / total[:, HEAD_DIM:]


def local(query_rows, key_value, out_weight, partners):
    groups = lax.axis_size("group")
    members = lax.axis_size("vf")
    local_views = members // FRAMES
    tokens, features = query_rows.shape[1:]
    heads = features // HEAD_DIM // groups
    parts = 2
    rows = tokens // parts
    view_count = groups * local_views
    shifts = [0]
    slots = []
    for offset in OFFSETS:
        if offset % local_views not in shifts:
            shifts.append(offset % local_views)
        slots.append(shifts.index(offset % local_views))
    relays = shifts[1:]
    order = sorted(range(1, groups), key=lambda r: abs(2 * r - groups))

    def kernel(
        partners_hbm, query_hbm, pair_hbm, weight_hbm, out_ref,
        partners_ref, queries, pairs, outs, gathered, weights, scores, total, squares,
        query_send, query_recv, pair_send, pair_recv, relay_send, relay_recv,
        out_send, out_recv, local_sem, weight_sem, partners_sem, below, above,
    ):
        mine = lax.axis_index("group")
        member = lax.axis_index("vf")
        view = member // FRAMES

        def partner(group, b):
            shifted = group * local_views + view + OFFSETS[b] + view_count
            return lax.rem(shifted, view_count)

        def gap(group, b):
            row = group * local_views + view
            gap = jnp.float32(FAR)
            for slot in range(partners_ref.shape[1]):
                gap = jnp.where(partners_ref[row, slot] == partner(group, b), 0.0, gap)
            return gap

        def columns(group, h):
            return pl.ds(pl.multiple_of((group * heads + h) * HEAD_DIM, HEAD_DIM), HEAD_DIM)

        def ahead(r):
            return lax.rem(mine + r, groups)

        def query_copy(h, r):
            return pltpu.make_async_remote_copy(
                src_ref=query_hbm.at[0, :, columns(ahead(r), h)],
                dst_ref=queries.at[h, mine],
                send_sem=query_send.at[h, r - 1],
                recv_sem=query_recv.at[h, r - 1],
                device_id={"group": ahead(r)},
                device_id_type=MESH,
            )

        def pair_copy(h, r):
            return pltpu.make_async_remote_copy(
                src_ref=pair_hbm.at[0, :, :, columns(ahead(r), h)],
                dst_ref=pairs.at[0, h, mine],
                send_sem=pair_send.at[h, r - 1],
                recv_sem=pair_recv.at[h, r - 1],
                device_id={"group": ahead(r)},
                device_id_type=MESH,
            )

        def relay_copy(h, r, i):
            origin = lax.rem(mine + groups - r, groups)
            source = pair_hbm.at[0, :, :, columns(mine, h)] if r == 0 else pairs.at[0, h, origin]
            return pltpu.make_async_remote_copy(
                src_ref=source,
                dst_ref=pairs.at[i + 1, h, origin],
                send_sem=relay_send.at[h, i, r],
                recv_sem=relay_recv.at[h, i, r],
                device_id={"vf": lax.rem(member + members - relays[i] * FRAMES, members)},
                device_id_type=MESH,
            )

        def own_copies(h):
            return (
                pltpu.make_async_copy(
                    query_hbm.at[0, :, columns(mine, h)], queries.at[h, mine], local_sem.at[h, 0]
                ),
                pltpu.make_async_copy(
                    pair_hbm.at[0, :, :, columns(mine, h)], pairs.at[0, h, mine], local_sem.at[h, 1]
                ),
            )

        def my_columns():
            return pl.ds(pl.multiple_of(mine * HEAD_DIM, HEAD_DIM), HEAD_DIM)

        def out_copy(h, r, part):
            strip = pl.ds(part * rows, rows)
            return pltpu.make_async_remote_copy(
                src_ref=outs.at[h, ahead(r), strip],
                dst_ref=gathered.at[h, strip, my_columns()],
                send_sem=out_send.at[h, r, part],
                recv_sem=out_recv.at[h, r, part],
                device_id={"group": ahead(r)},
                device_id_type=MESH,
            )

        def own_out(h):
            return pltpu.make_async_copy(
                outs.at[h, mine], gathered.at[h, :, my_columns()], local_sem.at[h, 2]
            )

        def weight_copy(h, group):
            return pltpu.make_async_copy(
                weight_hbm.at[pl.ds((group * heads + h) * HEAD_DIM, HEAD_DIM)],
                weights.at[h, pl.ds(group * HEAD_DIM, HEAD_DIM)],
                weight_sem.at[h, group],
            )

        def line_neighbours(act):
            @pl.when(mine > 0)
            def _():
                act(mine - 1)

            @pl.when(mine < groups - 1)
            def _():
                act(mine + 1)

        barrier = pltpu.get_barrier_semaphore()
        line_neighbours(
            lambda group: pl.semaphore_signal(barrier, inc=1, device_id={"group": group}, device_id_type=MESH)
        )
        for shift in relays:
            neighbour = lax.rem(member + shift * FRAMES, members)
            pl.semaphore_signal(barrier, inc=1, device_id={"vf": neighbour}, device_id_type=MESH)
        load_partners = pltpu.make_async_copy(partners_hbm, partners_ref, partners_sem)
        load_partners.start()
        for h in range(heads):
            for copy in own_copies(h):
                copy.start()
        beside = (mine > 0).astype(jnp.int32) + (mine < groups - 1).astype(jnp.int32)
        pl.semaphore_wait(barrier, beside + len(relays))

        def near(r):
            if r == 1:
                return (mine < groups - 1) | (mine > 0) if groups == 2 else mine < groups - 1
            return mine > 0 if r == groups - 1 else None

        for r in order:
            if near(r) is not None:
                pl.when(near(r))(pair_copy(0, r).start)
        for i in range(len(relays)):
            relay_copy(0, 0, i).start()

        for k in range(2, groups):
            @pl.when((mine - (k - 1) >= 0) & (mine + 1 < groups))
            def _():
                pl.semaphore_signal(below.at[k], inc=1, device_id={"group": mine + 1}, device_id_type=MESH)

            @pl.when((mine + (k - 1) < groups) & (mine > 0))
            def _():
                pl.semaphore_signal(above.at[k], inc=1, device_id={"group": mine - 1}, device_id_type=MESH)

            @pl.when(mine - k >= 0)
            def _():
                pl.semaphore_wait(below.at[k], 1)

            @pl.when(mine + k < groups)
            def _():
                pl.semaphore_wait(above.at[k], 1)

        for h in range(heads):
            for r in order:
                if h > 0 or near(r) is None:
                    pair_copy(h, r).start()
                else:
                    pl.when(jnp.logical_not(near(r)))(pair_copy(h, r).start)
            for r in order:
                query_copy(h, r).start()
            if h > 0:
                for i in range(len(relays)):
                    relay_copy(h, 0, i).start()
        for h in range(heads):
            for group in range(groups):
                weight_copy(h, group).start()
        load_partners.wait()

        @pl.loop(0, heads)
        def _(h):
            for r in order:
                pair_copy(h, r).wait_recv()
                for i in range(len(relays)):
                    relay_copy(h, r, i).start()
            for r in order:
                query_copy(h, r).wait_recv()
            for copy in own_copies(h):
                copy.wait()

            @pl.when(h == heads - 1)
            def _():
                for earlier in range(heads - 1):
                    for r in order:
                        for part in range(parts):
                            out_copy(earlier, r, part).start()

            for r in [0] + order:
                for i in range(len(relays)):
                    relay_copy(h, r, i).wait_recv()

            @pl.loop(0, groups)
            def _(step):
                r = lax.rem(step + 1, groups)
                target = ahead(r)

                def source(b):
                    return partner(target, b) // local_views

                sources = [source(b) for b in range(len(OFFSETS))]
                gaps = [gap(target, b) for b in range(len(OFFSETS))]
                for part in range(parts):
                    strip = pl.ds(part * rows, rows)
                    outs[h, target, strip] = attend_rows(
                        queries[h, target, strip],
                        lambda b: pairs[slots[b], h, sources[b], 0],
                        lambda b: pairs[slots[b], h, sources[b], 1],
                        lambda b: gaps[b],
                        scores.at[part],
                    ).astype(outs.dtype)

                @pl.when((step < groups - 1) & (h == heads - 1))
                def _():
                    for part in range(parts):
                        out_copy(h, r, part).start()

                @pl.when(step == groups - 1)
                def _():
                    own_out(h).start()

        total[...] = jnp.zeros_like(total)
        squares[...] = jnp.zeros_like(squares)
        width = groups * HEAD_DIM

        def square(h, strip):
            for c in range(0, width, HEAD_DIM):
                block = gathered[h, strip, c : c + HEAD_DIM].astype(jnp.float32)
                squares[strip] += block * block

        for h in range(heads):
            own_out(h).wait()
            for group in range(groups):
                weight_copy(h, group).wait()

        @pl.loop(0, heads - 1)
        def _(h):
            for r in range(1, groups):
                for part in range(parts):
                    out_copy(h, r, part).wait_recv()
            square(h, pl.ds(0, tokens))

            @pl.loop(0, features, step=width)
            def _(c):
                strip = pl.ds(pl.multiple_of(c, width), width)
                total[:, strip] += jnp.dot(
                    gathered[h], weights[h, :, strip], preferred_element_type=jnp.float32
                )

        last = heads - 1
        for part in range(parts):
            for r in range(1, groups):
                out_copy(last, r, part).wait_recv()
            strip = pl.ds(part * rows, rows)
            square(last, strip)
            mean = jnp.sum(squares[strip], axis=1, keepdims=True) * (1.0 / features)
            scale = lax.rsqrt(mean + 1e-06)
            for c in range(0, features, width):
                block = jnp.dot(
                    gathered[last, strip], weights[last, :, c : c + width], preferred_element_type=jnp.float32
                )
                out_ref[0, strip, c : c + width] = ((total[strip, c : c + width] + block) * scale).astype(
                    out_ref.dtype
                )

        @pl.loop(0, heads)
        def _(h):
            for r in range(1, groups):
                query_copy(h, r).wait_send()
                pair_copy(h, r).wait_send()
                for part in range(parts):
                    out_copy(h, r, part).wait_send()
            for r in range(groups):
                for i in range(len(relays)):
                    relay_copy(h, r, i).wait_send()

    hbm = pl.BlockSpec(memory_space=pl.ANY)
    dma = pltpu.SemaphoreType.DMA
    bf16 = jnp.bfloat16
    buffers = [
        ((heads, groups, tokens, HEAD_DIM), bf16),
        ((len(shifts), heads, groups, 2, tokens, HEAD_DIM), bf16),
        ((heads, groups, tokens, HEAD_DIM), bf16),
        ((heads, tokens, groups * HEAD_DIM), bf16),
        ((heads, groups * HEAD_DIM, features), bf16),
        ((parts, rows, tokens * len(OFFSETS)), jnp.float32),
        ((tokens, features), jnp.float32),
        ((tokens, HEAD_DIM), jnp.float32),
    ]
    held = sum(math.prod(shape) * jnp.dtype(dtype).itemsize for shape, dtype in buffers)
    return pl.pallas_call(
        kernel,
        out_shape=jax.ShapeDtypeStruct(query_rows.shape, bf16),
        in_specs=[hbm, hbm, hbm, hbm],
        out_specs=pl.BlockSpec(memory_space=pltpu.VMEM),
        scratch_shapes=[
            pltpu.SMEM(partners.shape, partners.dtype),
            *(pltpu.VMEM(shape, dtype) for shape, dtype in buffers),
            dma((heads, groups - 1)),
            dma((heads, groups - 1)),
            dma((heads, groups - 1)),
            dma((heads, groups - 1)),
            dma((heads, len(relays), groups)),
            dma((heads, len(relays), groups)),
            dma((heads, groups, parts)),
            dma((heads, groups, parts)),
            dma((heads, 3)),
            dma((heads, groups)),
            dma(()),
            pltpu.SemaphoreType.REGULAR((groups,)),
            pltpu.SemaphoreType.REGULAR((groups,)),
        ],
        compiler_params=pltpu.CompilerParams(
            collective_id=0, has_side_effects=True, vmem_limit_bytes=held + SPARE
        ),
    )(
        *(
            pltpu.with_memory_space_constraint(array, pltpu.HBM)
            for array in (partners, query_rows, key_value, out_weight)
        )
    )


def solution(mesh):
    placed = (P(("group", "vf"), None, None), P(("group", "vf"), None, None, None), P(), P())
    return jax.shard_map(
        local, mesh=mesh, in_specs=placed, out_specs=P(("group", "vf"), None, None), check_vma=False
    )
```

```python
import math

import jax
import jax.numpy as jnp
from jax import lax
from jax.experimental import pallas as pl
from jax.experimental.pallas import tpu as pltpu
from jax.sharding import PartitionSpec as P

HEADS = 12
HEAD_DIM = 128
FRAMES = 4
OFFSETS = (0, -3, -2, -1, 1, 2, 3)
SCALE = math.log2(math.e) / math.sqrt(HEAD_DIM)
FAR = 1e30
SPARE = 6 << 20
MESH = pl.DeviceIdType.MESH


def attend_rows(query, keys, values, gap, scores):
    tokens = keys(0).shape[0]
    running = None
    for b in range(len(OFFSETS)):
        block = lax.dot_general(
            query, keys(b), (((1,), (1,)), ((), ())), preferred_element_type=jnp.float32
        )
        scores[:, b * tokens : (b + 1) * tokens] = block
        lanes = block[:, :HEAD_DIM]
        for c in range(HEAD_DIM, tokens, HEAD_DIM):
            lanes = jnp.maximum(lanes, block[:, c : c + HEAD_DIM])
        running = lanes if b == 0 else jnp.maximum(running, lanes - gap(b))
    row_max = jnp.max(running, axis=1, keepdims=True) * SCALE
    total = None
    ones = jnp.ones((tokens, HEAD_DIM), jnp.bfloat16)
    for b in range(len(OFFSETS)):
        shift = row_max if b == 0 else row_max + gap(b)
        exponent = jnp.exp2(scores[:, b * tokens : (b + 1) * tokens] * SCALE - shift)
        part = jnp.dot(
            exponent.astype(jnp.bfloat16),
            jnp.concatenate([values(b), ones], axis=1),
            preferred_element_type=jnp.float32,
        )
        total = part if total is None else total + part
    return total[:, :HEAD_DIM] / total[:, HEAD_DIM:]


def local(query_rows, key_value, out_weight, partners):
    groups = lax.axis_size("group")
    members = lax.axis_size("vf")
    local_views = members // FRAMES
    tokens, features = query_rows.shape[1:]
    heads = features // HEAD_DIM // groups
    parts = 2
    rows = tokens // parts
    view_count = groups * local_views
    shifts = [0]
    slots = []
    for offset in OFFSETS:
        if offset % local_views not in shifts:
            shifts.append(offset % local_views)
        slots.append(shifts.index(offset % local_views))
    relays = shifts[1:]
    turns = range(groups - 1)
    inner_groups = ((groups - 1) // 2, groups // 2)

    def crosses(group, other):
        return (2 * group >= groups) != (2 * other >= groups)

    send_turns = [
        sorted(
            range(1, groups),
            key=lambda r: (not crosses(group, (group + r) % groups), -abs((group + r) % groups - group)),
        )
        for group in range(groups)
    ]
    wait_turns = [
        sorted(
            range(1, groups),
            key=lambda r: crosses(group, (group - r) % groups) and (group - r) % groups in inner_groups,
        )
        for group in range(groups)
    ]

    def kernel(
        partners_hbm, query_hbm, pair_hbm, weight_hbm, out_ref,
        partners_ref, queries, pairs, outs, gathered, weights, scores, total, squares,
        query_send, query_recv, pair_send, pair_recv, relay_send, relay_recv,
        out_send, out_recv, local_sem, weight_sem, partners_sem, below, above,
    ):
        mine = lax.axis_index("group")
        member = lax.axis_index("vf")
        view = member // FRAMES

        def partner(group, b):
            shifted = group * local_views + view + OFFSETS[b] + view_count
            return lax.rem(shifted, view_count)

        def gap(group, b):
            row = group * local_views + view
            gap = jnp.float32(FAR)
            for slot in range(partners_ref.shape[1]):
                gap = jnp.where(partners_ref[row, slot] == partner(group, b), 0.0, gap)
            return gap

        def columns(group, h):
            return pl.ds(pl.multiple_of((group * heads + h) * HEAD_DIM, HEAD_DIM), HEAD_DIM)

        def ahead(r):
            return lax.rem(mine + r, groups)

        def turn(table, i):
            return sum((mine == group).astype(jnp.int32) * table[group][i] for group in range(groups))

        to = [turn(send_turns, i) for i in turns]
        heard = [turn(wait_turns, i) for i in turns]
        inner = (mine == inner_groups[0]) | (mine == inner_groups[1])

        def query_copy(h, r):
            return pltpu.make_async_remote_copy(
                src_ref=query_hbm.at[0, :, columns(ahead(r), h)],
                dst_ref=queries.at[h, mine],
                send_sem=query_send.at[h, r - 1],
                recv_sem=query_recv.at[h, r - 1],
                device_id={"group": ahead(r)},
                device_id_type=MESH,
            )

        def pair_copy(h, r):
            return pltpu.make_async_remote_copy(
                src_ref=pair_hbm.at[0, :, :, columns(ahead(r), h)],
                dst_ref=pairs.at[0, h, mine],
                send_sem=pair_send.at[h, r - 1],
                recv_sem=pair_recv.at[h, r - 1],
                device_id={"group": ahead(r)},
                device_id_type=MESH,
            )

        def relay_copy(h, r, i):
            origin = lax.rem(mine + groups - r, groups)
            source = pair_hbm.at[0, :, :, columns(mine, h)] if isinstance(r, int) and r == 0 else pairs.at[0, h, origin]
            return pltpu.make_async_remote_copy(
                src_ref=source,
                dst_ref=pairs.at[i + 1, h, origin],
                send_sem=relay_send.at[h, i, r],
                recv_sem=relay_recv.at[h, i, r],
                device_id={"vf": lax.rem(member + members - relays[i] * FRAMES, members)},
                device_id_type=MESH,
            )

        def own_copies(h):
            return (
                pltpu.make_async_copy(
                    query_hbm.at[0, :, columns(mine, h)], queries.at[h, mine], local_sem.at[h, 0]
                ),
                pltpu.make_async_copy(
                    pair_hbm.at[0, :, :, columns(mine, h)], pairs.at[0, h, mine], local_sem.at[h, 1]
                ),
            )

        def my_columns():
            return pl.ds(pl.multiple_of(mine * HEAD_DIM, HEAD_DIM), HEAD_DIM)

        def out_copy(h, r, part):
            strip = pl.ds(part * rows, rows)
            return pltpu.make_async_remote_copy(
                src_ref=outs.at[h, ahead(r), strip],
                dst_ref=gathered.at[h, strip, my_columns()],
                send_sem=out_send.at[h, r, part],
                recv_sem=out_recv.at[h, r, part],
                device_id={"group": ahead(r)},
                device_id_type=MESH,
            )

        def own_out(h):
            return pltpu.make_async_copy(
                outs.at[h, mine], gathered.at[h, :, my_columns()], local_sem.at[h, 2]
            )

        def weight_copy(h, group):
            return pltpu.make_async_copy(
                weight_hbm.at[pl.ds((group * heads + h) * HEAD_DIM, HEAD_DIM)],
                weights.at[h, pl.ds(group * HEAD_DIM, HEAD_DIM)],
                weight_sem.at[h, group],
            )

        def line_neighbours(act):
            @pl.when(mine > 0)
            def _():
                act(mine - 1)

            @pl.when(mine < groups - 1)
            def _():
                act(mine + 1)

        barrier = pltpu.get_barrier_semaphore()
        line_neighbours(
            lambda group: pl.semaphore_signal(barrier, inc=1, device_id={"group": group}, device_id_type=MESH)
        )
        for shift in relays:
            neighbour = lax.rem(member + shift * FRAMES, members)
            pl.semaphore_signal(barrier, inc=1, device_id={"vf": neighbour}, device_id_type=MESH)
        load_partners = pltpu.make_async_copy(partners_hbm, partners_ref, partners_sem)
        load_partners.start()
        for h in range(heads):
            for copy in own_copies(h):
                copy.start()
        beside = (mine > 0).astype(jnp.int32) + (mine < groups - 1).astype(jnp.int32)
        pl.semaphore_wait(barrier, beside + len(relays))

        beside_above = mine < groups - 1
        beside_below = mine > 0

        def near(r):
            return ((r == 1) & beside_above) | ((r == groups - 1) & beside_below)

        for r in to:
            pl.when(near(r))(pair_copy(0, r).start)
        for i in range(len(relays)):
            relay_copy(0, 0, i).start()

        for k in range(2, groups):
            @pl.when((mine - (k - 1) >= 0) & (mine + 1 < groups))
            def _():
                pl.semaphore_signal(below.at[k], inc=1, device_id={"group": mine + 1}, device_id_type=MESH)

            @pl.when((mine + (k - 1) < groups) & (mine > 0))
            def _():
                pl.semaphore_signal(above.at[k], inc=1, device_id={"group": mine - 1}, device_id_type=MESH)

            @pl.when(mine - k >= 0)
            def _():
                pl.semaphore_wait(below.at[k], 1)

            @pl.when(mine + k < groups)
            def _():
                pl.semaphore_wait(above.at[k], 1)

        def send_head(h):
            for r in to:
                pair_copy(h, r).start()
            for r in to:
                query_copy(h, r).start()

        def send_outs(h):
            for r in to:
                for part in range(parts):
                    out_copy(h, r, part).start()

        for r in to:
            pl.when(jnp.logical_not(near(r)))(pair_copy(0, r).start)
        for r in to:
            query_copy(0, r).start()

        @pl.when(inner)
        def _():
            for h in range(1, heads):
                send_head(h)

        for h in range(1, heads):
            for i in range(len(relays)):
                relay_copy(h, 0, i).start()
        for h in range(heads):
            for group in range(groups):
                weight_copy(h, group).start()
        load_partners.wait()

        @pl.loop(0, heads)
        def _(h):
            for r in heard:
                pair_copy(h, r).wait_recv()
                for i in range(len(relays)):
                    relay_copy(h, r, i).start()
            for r in heard:
                query_copy(h, r).wait_recv()
            for copy in own_copies(h):
                copy.wait()

            @pl.when(jnp.logical_not(inner) & (h < heads - 1))
            def _():
                send_head(h + 1)

            @pl.when(jnp.logical_not(inner) & (h == heads - 1))
            def _():
                for earlier in range(heads - 1):
                    send_outs(earlier)

            for r in [0] + heard:
                for i in range(len(relays)):
                    relay_copy(h, r, i).wait_recv()

            @pl.loop(0, groups)
            def _(step):
                r = sum((step == i).astype(jnp.int32) * to[i] for i in turns)
                target = ahead(r)

                def source(b):
                    return partner(target, b) // local_views

                sources = [source(b) for b in range(len(OFFSETS))]
                gaps = [gap(target, b) for b in range(len(OFFSETS))]
                for part in range(parts):
                    strip = pl.ds(part * rows, rows)
                    outs[h, target, strip] = attend_rows(
                        queries[h, target, strip],
                        lambda b: pairs[slots[b], h, sources[b], 0],
                        lambda b: pairs[slots[b], h, sources[b], 1],
                        lambda b: gaps[b],
                        scores.at[part],
                    ).astype(outs.dtype)

                @pl.when((step < groups - 1) & (h == heads - 1))
                def _():
                    for part in range(parts):
                        out_copy(h, r, part).start()

                @pl.when(step == groups - 1)
                def _():
                    own_out(h).start()

            @pl.when(inner & (h < heads - 1))
            def _():
                send_outs(h)

        total[...] = jnp.zeros_like(total)
        squares[...] = jnp.zeros_like(squares)
        width = groups * HEAD_DIM

        def square(h, strip):
            for c in range(0, width, HEAD_DIM):
                block = gathered[h, strip, c : c + HEAD_DIM].astype(jnp.float32)
                squares[strip] += block * block

        for h in range(heads):
            own_out(h).wait()
            for group in range(groups):
                weight_copy(h, group).wait()

        @pl.loop(0, heads - 1)
        def _(h):
            for r in range(1, groups):
                for part in range(parts):
                    out_copy(h, r, part).wait_recv()
            square(h, pl.ds(0, tokens))

            @pl.loop(0, features, step=width)
            def _(c):
                strip = pl.ds(pl.multiple_of(c, width), width)
                total[:, strip] += jnp.dot(
                    gathered[h], weights[h, :, strip], preferred_element_type=jnp.float32
                )

        last = heads - 1
        for part in range(parts):
            for r in range(1, groups):
                out_copy(last, r, part).wait_recv()
            strip = pl.ds(part * rows, rows)
            square(last, strip)
            mean = jnp.sum(squares[strip], axis=1, keepdims=True) * (1.0 / features)
            scale = lax.rsqrt(mean + 1e-06)
            for c in range(0, features, width):
                block = jnp.dot(
                    gathered[last, strip], weights[last, :, c : c + width], preferred_element_type=jnp.float32
                )
                out_ref[0, strip, c : c + width] = ((total[strip, c : c + width] + block) * scale).astype(
                    out_ref.dtype
                )

        @pl.loop(0, heads)
        def _(h):
            for r in range(1, groups):
                query_copy(h, r).wait_send()
                pair_copy(h, r).wait_send()
                for part in range(parts):
                    out_copy(h, r, part).wait_send()
            for r in range(groups):
                for i in range(len(relays)):
                    relay_copy(h, r, i).wait_send()

    hbm = pl.BlockSpec(memory_space=pl.ANY)
    dma = pltpu.SemaphoreType.DMA
    bf16 = jnp.bfloat16
    buffers = [
        ((heads, groups, tokens, HEAD_DIM), bf16),
        ((len(shifts), heads, groups, 2, tokens, HEAD_DIM), bf16),
        ((heads, groups, tokens, HEAD_DIM), bf16),
        ((heads, tokens, groups * HEAD_DIM), bf16),
        ((heads, groups * HEAD_DIM, features), bf16),
        ((parts, rows, tokens * len(OFFSETS)), jnp.float32),
        ((tokens, features), jnp.float32),
        ((tokens, HEAD_DIM), jnp.float32),
    ]
    held = sum(math.prod(shape) * jnp.dtype(dtype).itemsize for shape, dtype in buffers)
    return pl.pallas_call(
        kernel,
        out_shape=jax.ShapeDtypeStruct(query_rows.shape, bf16),
        in_specs=[hbm, hbm, hbm, hbm],
        out_specs=pl.BlockSpec(memory_space=pltpu.VMEM),
        scratch_shapes=[
            pltpu.SMEM(partners.shape, partners.dtype),
            *(pltpu.VMEM(shape, dtype) for shape, dtype in buffers),
            dma((heads, groups - 1)),
            dma((heads, groups - 1)),
            dma((heads, groups - 1)),
            dma((heads, groups - 1)),
            dma((heads, len(relays), groups)),
            dma((heads, len(relays), groups)),
            dma((heads, groups, parts)),
            dma((heads, groups, parts)),
            dma((heads, 3)),
            dma((heads, groups)),
            dma(()),
            pltpu.SemaphoreType.REGULAR((groups,)),
            pltpu.SemaphoreType.REGULAR((groups,)),
        ],
        compiler_params=pltpu.CompilerParams(
            collective_id=0, has_side_effects=True, vmem_limit_bytes=held + SPARE
        ),
    )(
        *(
            pltpu.with_memory_space_constraint(array, pltpu.HBM)
            for array in (partners, query_rows, key_value, out_weight)
        )
    )


def solution(mesh):
    placed = (P(("group", "vf"), None, None), P(("group", "vf"), None, None, None), P(), P())
    return jax.shard_map(
        local, mesh=mesh, in_specs=placed, out_specs=P(("group", "vf"), None, None), check_vma=False
    )
```

```python
import math

import jax
import jax.numpy as jnp
from jax import lax
from jax.experimental import pallas as pl
from jax.experimental.pallas import tpu as pltpu
from jax.sharding import PartitionSpec as P

HEADS = 12
HEAD_DIM = 128
FRAMES = 4
OFFSETS = (0, -3, -2, -1, 1, 2, 3)
SCALE = math.log2(math.e) / math.sqrt(HEAD_DIM)
FAR = 1e30
SPARE = 6 << 20
MESH = pl.DeviceIdType.MESH


def attend_rows(query, keys, values, gap, scores):
    tokens = keys(0).shape[0]
    running = None
    for b in range(len(OFFSETS)):
        block = lax.dot_general(
            query, keys(b), (((1,), (1,)), ((), ())), preferred_element_type=jnp.float32
        )
        scores[:, b * tokens : (b + 1) * tokens] = block
        lanes = block[:, :HEAD_DIM]
        for c in range(HEAD_DIM, tokens, HEAD_DIM):
            lanes = jnp.maximum(lanes, block[:, c : c + HEAD_DIM])
        running = lanes if b == 0 else jnp.maximum(running, lanes - gap(b))
    row_max = jnp.max(running, axis=1, keepdims=True) * SCALE
    total = None
    ones = jnp.ones((tokens, HEAD_DIM), jnp.bfloat16)
    for b in range(len(OFFSETS)):
        shift = row_max if b == 0 else row_max + gap(b)
        exponent = jnp.exp2(scores[:, b * tokens : (b + 1) * tokens] * SCALE - shift)
        part = jnp.dot(
            exponent.astype(jnp.bfloat16),
            jnp.concatenate([values(b), ones], axis=1),
            preferred_element_type=jnp.float32,
        )
        total = part if total is None else total + part
    return total[:, :HEAD_DIM] / total[:, HEAD_DIM:]


def local(query_rows, key_value, out_weight, partners):
    groups = lax.axis_size("group")
    members = lax.axis_size("vf")
    local_views = members // FRAMES
    tokens, features = query_rows.shape[1:]
    heads = features // HEAD_DIM // groups
    parts = 2
    rows = tokens // parts
    view_count = groups * local_views
    shifts = [0]
    slots = []
    for offset in OFFSETS:
        if offset % local_views not in shifts:
            shifts.append(offset % local_views)
        slots.append(shifts.index(offset % local_views))
    relays = shifts[1:]
    turns = range(groups - 1)
    inner_groups = ((groups - 1) // 2, groups // 2)

    def crosses(group, other):
        return (2 * group >= groups) != (2 * other >= groups)

    def towards_middle(group):
        return group + 1 if 2 * group + 1 < groups else group - 1 if 2 * group + 1 > groups else -1

    parents = [towards_middle(group) for group in range(groups)]
    children = [[other for other in range(groups) if parents[other] == group] for group in range(groups)]

    send_turns = [
        sorted(
            range(1, groups),
            key=lambda r: (not crosses(group, (group + r) % groups), -abs((group + r) % groups - group)),
        )
        for group in range(groups)
    ]
    wait_turns = [
        sorted(
            range(1, groups),
            key=lambda r: crosses(group, (group - r) % groups) and (group - r) % groups in inner_groups,
        )
        for group in range(groups)
    ]

    def kernel(
        partners_hbm, query_hbm, pair_hbm, weight_hbm, out_ref,
        partners_ref, queries, pairs, outs, gathered, weights, scores, total, squares,
        query_send, query_recv, pair_send, pair_recv, relay_send, relay_recv,
        out_send, out_recv, local_sem, weight_sem, partners_sem, below, above,
    ):
        mine = lax.axis_index("group")
        member = lax.axis_index("vf")
        view = member // FRAMES

        def partner(group, b):
            shifted = group * local_views + view + OFFSETS[b] + view_count
            return lax.rem(shifted, view_count)

        def gap(group, b):
            row = group * local_views + view
            gap = jnp.float32(FAR)
            for slot in range(partners_ref.shape[1]):
                gap = jnp.where(partners_ref[row, slot] == partner(group, b), 0.0, gap)
            return gap

        def columns(group, h):
            return pl.ds(pl.multiple_of((group * heads + h) * HEAD_DIM, HEAD_DIM), HEAD_DIM)

        def ahead(r):
            return lax.rem(mine + r, groups)

        def turn(table, i):
            return sum((mine == group).astype(jnp.int32) * table[group][i] for group in range(groups))

        to = [turn(send_turns, i) for i in turns]
        heard = [turn(wait_turns, i) for i in turns]
        parent = sum((mine == group).astype(jnp.int32) * parents[group] for group in range(groups))
        inner = (mine == inner_groups[0]) | (mine == inner_groups[1])

        def query_copy(h, r):
            return pltpu.make_async_remote_copy(
                src_ref=query_hbm.at[0, :, columns(ahead(r), h)],
                dst_ref=queries.at[h, mine],
                send_sem=query_send.at[h, r - 1],
                recv_sem=query_recv.at[h, r - 1],
                device_id={"group": ahead(r)},
                device_id_type=MESH,
            )

        def pair_copy(h, r):
            return pltpu.make_async_remote_copy(
                src_ref=pair_hbm.at[0, :, :, columns(ahead(r), h)],
                dst_ref=pairs.at[0, h, mine],
                send_sem=pair_send.at[h, r - 1],
                recv_sem=pair_recv.at[h, r - 1],
                device_id={"group": ahead(r)},
                device_id_type=MESH,
            )

        def relay_copy(h, r, i):
            origin = lax.rem(mine + groups - r, groups)
            source = pair_hbm.at[0, :, :, columns(mine, h)] if isinstance(r, int) and r == 0 else pairs.at[0, h, origin]
            return pltpu.make_async_remote_copy(
                src_ref=source,
                dst_ref=pairs.at[i + 1, h, origin],
                send_sem=relay_send.at[h, i, r],
                recv_sem=relay_recv.at[h, i, r],
                device_id={"vf": lax.rem(member + members - relays[i] * FRAMES, members)},
                device_id_type=MESH,
            )

        def own_copies(h):
            return (
                pltpu.make_async_copy(
                    query_hbm.at[0, :, columns(mine, h)], queries.at[h, mine], local_sem.at[h, 0]
                ),
                pltpu.make_async_copy(
                    pair_hbm.at[0, :, :, columns(mine, h)], pairs.at[0, h, mine], local_sem.at[h, 1]
                ),
            )

        def my_columns():
            return pl.ds(pl.multiple_of(mine * HEAD_DIM, HEAD_DIM), HEAD_DIM)

        def out_copy(h, r, part):
            strip = pl.ds(part * rows, rows)
            return pltpu.make_async_remote_copy(
                src_ref=outs.at[h, ahead(r), strip],
                dst_ref=gathered.at[h, strip, my_columns()],
                send_sem=out_send.at[h, r, part],
                recv_sem=out_recv.at[h, r, part],
                device_id={"group": ahead(r)},
                device_id_type=MESH,
            )

        def own_out(h):
            return pltpu.make_async_copy(
                outs.at[h, mine], gathered.at[h, :, my_columns()], local_sem.at[h, 2]
            )

        def weight_copy(h, group):
            return pltpu.make_async_copy(
                weight_hbm.at[pl.ds((group * heads + h) * HEAD_DIM, HEAD_DIM)],
                weights.at[h, pl.ds(group * HEAD_DIM, HEAD_DIM)],
                weight_sem.at[h, group],
            )

        def tell(semaphore, group):
            pl.semaphore_signal(semaphore, inc=1, device_id={"group": group}, device_id_type=MESH)

        def among(members_of):
            return sum(((mine == group).astype(jnp.int32) for group in members_of), jnp.int32(0)) > 0

        barrier = pltpu.get_barrier_semaphore()
        for step in (-1, 1):
            telling = [g for g in range(groups) if g + step in children[g]]
            pl.when(among(telling))(lambda step=step: tell(barrier, mine + step))
        for shift in relays:
            neighbour = lax.rem(member + shift * FRAMES, members)
            pl.semaphore_signal(barrier, inc=1, device_id={"vf": neighbour}, device_id_type=MESH)
        load_partners = pltpu.make_async_copy(partners_hbm, partners_ref, partners_sem)
        load_partners.start()
        for h in range(heads):
            for copy in own_copies(h):
                copy.start()
        pl.semaphore_wait(barrier, (parent >= 0).astype(jnp.int32) + len(relays))

        def near(r):
            return ahead(r) == parent

        for r in to:
            pl.when(near(r))(pair_copy(0, r).start)
        for i in range(len(relays)):
            relay_copy(0, 0, i).start()

        for step, semaphore in ((1, below), (-1, above)):
            reporting = [g for g in range(groups) if parents[g] == g + step and parents[g + step] != g]
            hearing = [g + step for g in reporting]
            pl.when(among(reporting))(lambda step=step, semaphore=semaphore: tell(semaphore.at[1], mine + step))
            pl.when(among(hearing))(lambda semaphore=semaphore: pl.semaphore_wait(semaphore.at[1], 1))

        for k in range(2, groups):
            @pl.when((mine - (k - 1) >= 0) & (mine + 1 < groups))
            def _():
                tell(below.at[k], mine + 1)

            @pl.when((mine + (k - 1) < groups) & (mine > 0))
            def _():
                tell(above.at[k], mine - 1)

            @pl.when(mine - k >= 0)
            def _():
                pl.semaphore_wait(below.at[k], 1)

            @pl.when(mine + k < groups)
            def _():
                pl.semaphore_wait(above.at[k], 1)

        def send_head(h):
            for r in to:
                pair_copy(h, r).start()
            for r in to:
                query_copy(h, r).start()

        def send_outs(h):
            for r in to:
                for part in range(parts):
                    out_copy(h, r, part).start()

        for r in to:
            pl.when(jnp.logical_not(near(r)))(pair_copy(0, r).start)
        for r in to:
            query_copy(0, r).start()

        @pl.when(inner)
        def _():
            for h in range(1, heads):
                send_head(h)

        for h in range(1, heads):
            for i in range(len(relays)):
                relay_copy(h, 0, i).start()
        for h in range(heads):
            for group in range(groups):
                weight_copy(h, group).start()
        load_partners.wait()

        @pl.loop(0, heads)
        def _(h):
            for r in heard:
                pair_copy(h, r).wait_recv()
                for i in range(len(relays)):
                    relay_copy(h, r, i).start()
            for r in heard:
                query_copy(h, r).wait_recv()
            for copy in own_copies(h):
                copy.wait()

            @pl.when(jnp.logical_not(inner) & (h < heads - 1))
            def _():
                send_head(h + 1)

            @pl.when(jnp.logical_not(inner) & (h == heads - 1))
            def _():
                for earlier in range(heads - 1):
                    send_outs(earlier)

            for r in [0] + heard:
                for i in range(len(relays)):
                    relay_copy(h, r, i).wait_recv()

            @pl.loop(0, groups)
            def _(step):
                r = sum((step == i).astype(jnp.int32) * to[i] for i in turns)
                target = ahead(r)

                def source(b):
                    return partner(target, b) // local_views

                sources = [source(b) for b in range(len(OFFSETS))]
                gaps = [gap(target, b) for b in range(len(OFFSETS))]
                for part in range(parts):
                    strip = pl.ds(part * rows, rows)
                    outs[h, target, strip] = attend_rows(
                        queries[h, target, strip],
                        lambda b: pairs[slots[b], h, sources[b], 0],
                        lambda b: pairs[slots[b], h, sources[b], 1],
                        lambda b: gaps[b],
                        scores.at[part],
                    ).astype(outs.dtype)

                @pl.when((step < groups - 1) & (h == heads - 1))
                def _():
                    for part in range(parts):
                        out_copy(h, r, part).start()

                @pl.when(step == groups - 1)
                def _():
                    own_out(h).start()

            @pl.when(inner & (h < heads - 1))
            def _():
                send_outs(h)

        total[...] = jnp.zeros_like(total)
        squares[...] = jnp.zeros_like(squares)
        width = groups * HEAD_DIM

        def square(h, strip):
            for c in range(0, width, HEAD_DIM):
                block = gathered[h, strip, c : c + HEAD_DIM].astype(jnp.float32)
                squares[strip] += block * block

        for h in range(heads):
            own_out(h).wait()
            for group in range(groups):
                weight_copy(h, group).wait()

        @pl.loop(0, heads - 1)
        def _(h):
            for r in range(1, groups):
                for part in range(parts):
                    out_copy(h, r, part).wait_recv()
            square(h, pl.ds(0, tokens))

            @pl.loop(0, features, step=width)
            def _(c):
                strip = pl.ds(pl.multiple_of(c, width), width)
                total[:, strip] += jnp.dot(
                    gathered[h], weights[h, :, strip], preferred_element_type=jnp.float32
                )

        last = heads - 1
        for part in range(parts):
            for r in range(1, groups):
                out_copy(last, r, part).wait_recv()
            strip = pl.ds(part * rows, rows)
            square(last, strip)
            mean = jnp.sum(squares[strip], axis=1, keepdims=True) * (1.0 / features)
            scale = lax.rsqrt(mean + 1e-06)
            for c in range(0, features, width):
                block = jnp.dot(
                    gathered[last, strip], weights[last, :, c : c + width], preferred_element_type=jnp.float32
                )
                out_ref[0, strip, c : c + width] = ((total[strip, c : c + width] + block) * scale).astype(
                    out_ref.dtype
                )

        @pl.loop(0, heads)
        def _(h):
            for r in range(1, groups):
                query_copy(h, r).wait_send()
                pair_copy(h, r).wait_send()
                for part in range(parts):
                    out_copy(h, r, part).wait_send()
            for r in range(groups):
                for i in range(len(relays)):
                    relay_copy(h, r, i).wait_send()

    hbm = pl.BlockSpec(memory_space=pl.ANY)
    dma = pltpu.SemaphoreType.DMA
    bf16 = jnp.bfloat16
    buffers = [
        ((heads, groups, tokens, HEAD_DIM), bf16),
        ((len(shifts), heads, groups, 2, tokens, HEAD_DIM), bf16),
        ((heads, groups, tokens, HEAD_DIM), bf16),
        ((heads, tokens, groups * HEAD_DIM), bf16),
        ((heads, groups * HEAD_DIM, features), bf16),
        ((parts, rows, tokens * len(OFFSETS)), jnp.float32),
        ((tokens, features), jnp.float32),
        ((tokens, HEAD_DIM), jnp.float32),
    ]
    held = sum(math.prod(shape) * jnp.dtype(dtype).itemsize for shape, dtype in buffers)
    return pl.pallas_call(
        kernel,
        out_shape=jax.ShapeDtypeStruct(query_rows.shape, bf16),
        in_specs=[hbm, hbm, hbm, hbm],
        out_specs=pl.BlockSpec(memory_space=pltpu.VMEM),
        scratch_shapes=[
            pltpu.SMEM(partners.shape, partners.dtype),
            *(pltpu.VMEM(shape, dtype) for shape, dtype in buffers),
            dma((heads, groups - 1)),
            dma((heads, groups - 1)),
            dma((heads, groups - 1)),
            dma((heads, groups - 1)),
            dma((heads, len(relays), groups)),
            dma((heads, len(relays), groups)),
            dma((heads, groups, parts)),
            dma((heads, groups, parts)),
            dma((heads, 3)),
            dma((heads, groups)),
            dma(()),
            pltpu.SemaphoreType.REGULAR((groups,)),
            pltpu.SemaphoreType.REGULAR((groups,)),
        ],
        compiler_params=pltpu.CompilerParams(
            collective_id=0, has_side_effects=True, vmem_limit_bytes=held + SPARE
        ),
    )(
        *(
            pltpu.with_memory_space_constraint(array, pltpu.HBM)
            for array in (partners, query_rows, key_value, out_weight)
        )
    )


def solution(mesh):
    placed = (P(("group", "vf"), None, None), P(("group", "vf"), None, None, None), P(), P())
    return jax.shard_map(
        local, mesh=mesh, in_specs=placed, out_specs=P(("group", "vf"), None, None), check_vma=False
    )
```
